128 devices in a mesh: row: 8 (over z_lo, x), col: 16 (over z_hi, y, core).
Axes of the slice: x: 4, y: 4, z: 4 (z_hi: 2, z_lo: 2; z = z_hi * 2 + z_lo), core: 2. Of those that a mesh axis runs over, the one named last changes fastest.
Arguments:
- trailing: float32 [12288, 24576], P('row', 'col'), may hold values from -6 to 6
- u_factors: float32 [16, 1536, 640], P('col', 'row'), may hold values from -0.5 to 0.5
- v_factors: float32 [16, 1536, 640], P('col', 'row'), may hold values from -0.5 to 0.5
- ranks: int32 [16, 4], replicated, may hold values from 96 to 160
- panel_sims: float32 [6144, 2048], P('col', 'row'), may hold values from -2 to 2
- trailing_sims: float32 [24576, 2048], P('col', 'row'), may hold values from -6 to 6
Outputs:
- updated: float32 [12288, 24576], P('row', 'col')
- conditioned: float32 [24576, 2048], P('col', 'row')
The draws below stay inside these ranges and needn't reach their ends.
All inputs are finite; a program needn't handle non-finite values.
Results may differ from the reference program's by a relative error of at most 0.00005.
Values sent between devices are 32-bit elements; how exact they have to be, the bound alone decides.
No kernel may reach another device: no remote copies, remote signals or barrier semaphores. Data moves between devices by JAX's collectives and lax.ppermute only.
A program may use at most 128 MiB of HBM per device.

```python
import jax
import jax.numpy as jnp
from jax import lax

B = 1536
K = 160
P_SIZE = 4
TILE_ROWS = 8
TILE_COLS = 16
SIMS = 2048
N_ROW = 8
N_COL = 16


def plant(array, own_key, low, high):
    dims = array.shape
    spot = [jax.random.randint(jax.random.fold_in(own_key, axis), (), 0, dims[axis]) for axis in range(len(dims))]
    array = array.at[tuple(spot)].set(low)
    longest = dims.index(max(dims))
    spot[longest] = (spot[longest] + 1) % dims[longest]
    return array.at[tuple(spot)].set(high)


def steps_of(own_key, dims, pieces, smallest, largest):
    def one(dim, shards_of):
        heights = jax.random.uniform(jax.random.fold_in(jax.random.fold_in(own_key, 6), dim), (shards_of,), jnp.float32, smallest / len(pieces), largest / len(pieces))
        return jnp.repeat(jnp.exp(heights), dims[dim] // shards_of).reshape((-1,) + (1,) * (len(dims) - dim - 1))

    loudness = one(*pieces[0])
    for cut in pieces[1:]:
        loudness = loudness * one(*cut)
    return loudness


def normal_values(rng, shape, spread, most, pieces=(), kind=jnp.bfloat16):
    result = jax.random.normal(rng, shape, jnp.float32) * spread
    if len(pieces) > 0:
        result = steps_of(rng, shape, pieces, -0.22, 0.18) * result
    return jnp.clip(result, min=-most, max=most).astype(kind)


def setup_inputs(seed: int = 0) -> dict:
    arg_keys = jax.random.split(jax.random.key(seed), 7)
    trailing = normal_values(arg_keys[0], (TILE_ROWS * B, TILE_COLS * B), 1.0, 6.0, ((0, 8), (1, 16)), jnp.float32)
    u_factors = normal_values(arg_keys[1], (TILE_COLS, B, P_SIZE * K), K ** -0.5, 0.5, ((0, 16), (1, 8)), jnp.float32)
    v_factors = normal_values(arg_keys[2], (TILE_COLS, B, P_SIZE * K), 0.08, 0.5, ((0, 16), (1, 8)), jnp.float32)
    ranks = plant(jax.random.randint(arg_keys[3], (TILE_COLS, P_SIZE), K * 3 // 5, K + 1), jax.random.fold_in(arg_keys[3], 1), K * 3 // 5, K).astype(jnp.int32)
    panel_sims = normal_values(arg_keys[4], (P_SIZE * B, SIMS), 0.25, 2.0, ((0, 16), (1, 8)), jnp.float32)
    trailing_sims = normal_values(arg_keys[5], (TILE_COLS * B, SIMS), 1.0, 6.0, ((0, 16), (1, 8)), jnp.float32)
    return dict(trailing=trailing, u_factors=u_factors, v_factors=v_factors, ranks=ranks, panel_sims=panel_sims, trailing_sims=trailing_sims)


def reference(trailing, u_factors, v_factors, ranks, panel_sims, trailing_sims):
    precise = lax.Precision.HIGHEST
    levels = jnp.arange(K, dtype=jnp.int32)
    keep_mask = (levels[None, None, :] < ranks[:, :, None]).astype(jnp.float32).reshape(N_COL, P_SIZE * K)
    v_masked = v_factors * keep_mask[:, None, :]
    u_split = u_factors.reshape(N_COL, B, P_SIZE, K)
    v_split = v_masked.reshape(N_COL, B, P_SIZE, K)

    def row_update(row_tile):
        core_block = jnp.einsum('bpk,cbpl->cpkl', v_split[row_tile], v_split, precision=precise)
        left_part = jnp.einsum('bpk,cpkl->cbpl', u_split[row_tile], core_block, precision=precise)
        left_part = left_part.reshape(N_COL, B, P_SIZE * K)
        return jnp.einsum('cbj,cdj->bcd', left_part, u_factors, precision=precise).reshape(B, N_COL * B)

    decrease = lax.map(row_update, jnp.arange(N_ROW, dtype=jnp.int32))
    updated = trailing - decrease.reshape(N_ROW * B, N_COL * B)
    panel_split = panel_sims.reshape(P_SIZE, B, panel_sims.shape[1])
    weights = jnp.einsum('cbpk,pbs->cpks', v_split, panel_split, precision=precise)
    lowered = jnp.einsum('cbpk,cpks->cbs', u_split, weights, precision=precise)
    conditioned = trailing_sims - lowered.reshape(N_COL * B, panel_sims.shape[1])
    return updated, conditioned
```

```python
import jax
import jax.numpy as jnp
from jax import lax
from jax.experimental import pallas as pl
from jax.experimental.pallas import tpu as pltpu
from jax.sharding import PartitionSpec as P

B, K, PANELS, SIMS_LOCAL = 1536, 160, 4, 256
J = PANELS * K
BR = B // 8
XR = 384
WIN = 256


def pairs(move):
    out = []
    for i in range(128):
        row, col = divmod(i, 16)
        zl, x = divmod(row, 4)
        zh, yc = divmod(col, 8)
        y, core = divmod(yc, 2)
        to = move(zl, x, zh, y, core)
        if to is not None:
            zl, x, zh, y, core = to
            out.append((i, (zl * 4 + x % 4) * 16 + zh * 8 + (y % 4) * 2 + core))
    return out


X_UP = pairs(lambda zl, x, zh, y, c: (zl, x + 1, zh, y, c))
X_DOWN = pairs(lambda zl, x, zh, y, c: (zl, x - 1, zh, y, c))
Y_UP = pairs(lambda zl, x, zh, y, c: (zl, x, zh, y + 1, c))
Y_DOWN = pairs(lambda zl, x, zh, y, c: (zl, x, zh, y - 1, c))
Z_LOW = pairs(lambda zl, x, zh, y, c: (1 - zl, x, zh, y, c))
Z_HIGH = pairs(lambda zl, x, zh, y, c: (zl, x, 1 - zh, y, c))
CORE = pairs(lambda zl, x, zh, y, c: (zl, x, zh, y, 1 - c))
SPREAD = pairs(lambda zl, x, zh, y, c: None if zh else (zl, x, 1, y, c))
TO_ROW = pairs(lambda zl, x, zh, y, c: ((2 * y + c) // 4, (2 * y + c) % 4, zh, x, zl))


def send(value, where):
    return lax.ppermute(value, ("row", "col"), where)


def ring_gather(own, across, up, down):
    half = own.shape[0] // 2
    below = send(own, up)
    above = send(own, down)
    far = send(own, across)
    far1 = send(below[:half], up)
    far2 = send(above[half:], down)
    pair_below = send(far, up)
    pair_above = send(far, down)
    pair1 = send(pair_below[:half], up)
    pair2 = send(pair_above[half:], down)
    return [
        (0, 0, 0, own), (0, 3, 0, below), (0, 1, 0, above), (1, 0, 0, far),
        (0, 2, 0, far1), (0, 2, half, far2), (1, 3, 0, pair_below), (1, 1, 0, pair_above),
        (1, 2, 0, pair1), (1, 2, half, pair2),
    ]


def split(a):
    high = a.astype(jnp.bfloat16)
    return high, (a - high.astype(jnp.float32)).astype(jnp.bfloat16)


def dot3(a, b, dims):
    ah, al = a
    bh, bl = b
    one = lambda s, t: lax.dot_general(s, t, (dims, ((), ())), preferred_element_type=jnp.float32)
    return one(ah, bh) + (one(ah, bl) + one(al, bh))


TN = ((0,), (0,))
NT = ((1,), (1,))
NN = ((1,), (0,))


def factor_rows(pos, pair, ring, off):
    return pl.multiple_of(((pos[0] ^ pair) * 4 + lax.rem(pos[1] + ring, 4)) * BR + off, 8)


def piece_rows(pos, core, pair, ring, off):
    return pl.multiple_of((core * 4 + lax.rem(pos[3] + ring, 4)) * BR + (pos[2] ^ pair) * (BR // 2) + off, 8)


def sims_rows(pos, core, pair, ring, off):
    return pl.multiple_of(((pos[2] ^ pair) * 8 + lax.rem(pos[3] + ring, 4) * 2 + core) * XR + off, 8)


def run_all(copies):
    for c in copies:
        c.start()
    for c in copies:
        c.wait()


def small_products(offsets_f, offsets_p, offsets_x, n_f):
    def body(pos, keep_c, keep_r, mine_p, other_p, mine_x, other_x, *rest):
        blocks = rest[:n_f]
        core_out, weight_out, vc, vr, xs, sem = rest[n_f:]
        copies = []

        def add(src, dst):
            copies.append(pltpu.make_async_copy(src, dst, sem.at[len(copies)]))

        for (pair, ring, off, n), ref in zip(offsets_f, blocks):
            add(ref.at[:, pl.ds(0, J)], vc.at[pl.ds(factor_rows(pos, pair, ring, off), n), :])
        for core, ref in ((pos[4], mine_p), (1 - pos[4], other_p)):
            at = 0
            for pair, ring, off, n in offsets_p:
                add(ref.at[pl.ds(at, n), pl.ds(0, J)], vr.at[pl.ds(piece_rows(pos, core, pair, ring, off), n), :])
                at += n
        for core, ref in ((pos[4], mine_x), (1 - pos[4], other_x)):
            at = 0
            for pair, ring, off, n in offsets_x:
                add(ref.at[pl.ds(at, n), :], xs.at[pl.ds(sims_rows(pos, core, pair, ring, off), n), :])
                at += n
        run_all(copies)
        weight_out[...] = jnp.zeros_like(weight_out)
        for p in range(PANELS):
            lanes = pl.ds(128 * p, WIN)
            left = split(vc[:, lanes])
            core = dot3(left, split(vr[:, lanes]), TN)
            weights = dot3(left, split(xs[pl.ds(B * p, B), :]), TN)
            rows = lax.broadcasted_iota(jnp.int32, (WIN, WIN), 0) + (128 * p - K * p)
            cols = lax.broadcasted_iota(jnp.int32, (WIN, WIN), 1) + (128 * p - K * p)
            live = (rows >= 0) & (rows < keep_c[p])
            core_out[p] = jnp.where(live & (cols >= 0) & (cols < keep_r[p]), core, 0.0)
            weight_out[lanes, :] += jnp.where(live, weights, 0.0)

    return body


def large_products(offsets_f, offsets_p, n_f, steps):
    tall = B // steps

    def body(pos, trailing, sims, core_in, weights, mine_p, other_p, *rest):
        blocks = rest[:n_f]
        updated, conditioned, uc, ur, uch, ucl, sem = rest[n_f:]
        i = pl.program_id(0)

        @pl.when(i == 0)
        def _():
            copies = []

            def add(src, dst):
                copies.append(pltpu.make_async_copy(src, dst, sem.at[len(copies)]))

            for (pair, ring, off, n), ref in zip(offsets_f, blocks):
                add(ref.at[:, pl.ds(J, J)], uc.at[pl.ds(factor_rows(pos, pair, ring, off), n), :])
            for core, ref in ((pos[4], mine_p), (1 - pos[4], other_p)):
                at = 0
                for pair, ring, off, n in offsets_p:
                    add(ref.at[pl.ds(at, n), pl.ds(J, J)], ur.at[pl.ds(piece_rows(pos, core, pair, ring, off), n), :])
                    at += n
            run_all(copies)
            uch[...], ucl[...] = split(uc[...])

        here = pl.ds(pl.multiple_of(i * tall, 128), tall)
        pieces = [dot3(split(ur[here, pl.ds(128 * p, WIN)]), split(core_in[p]), NT) for p in range(PANELS)]
        left = jnp.concatenate(
            [pieces[0][:, :128]]
            + [pieces[p][:, 128:] + pieces[p + 1][:, :128] for p in range(PANELS - 1)]
            + [pieces[-1][:, 128:]], axis=1)
        updated[...] = trailing[...] - dot3(split(left), (uch[...], ucl[...]), NT)
        conditioned[...] = sims[...] - dot3((uch[here, :], ucl[here, :]), split(weights[...]), NN)

    return body


def on_device(trailing, u_factors, v_factors, ranks, panel_sims, trailing_sims):
    row = lax.axis_index("row")
    col = lax.axis_index("col")
    pos = jnp.stack([row // 4, row % 4, col // 8, (col // 2) % 4, col % 2]).astype(jnp.int32)
    keep_c = lax.dynamic_index_in_dim(ranks, col, 0, keepdims=False)
    keep_r = lax.dynamic_index_in_dim(ranks, row, 0, keepdims=False)

    factors = jnp.concatenate([v_factors[0], u_factors[0]], axis=1)
    moved = send(factors[BR // 2:], SPREAD)
    piece = send(jnp.where(pos[2] == 0, factors[:BR // 2], moved), TO_ROW)
    blocks = ring_gather(factors, Z_LOW, X_UP, X_DOWN)
    sims = ring_gather(panel_sims, Z_HIGH, Y_UP, Y_DOWN)
    pieces = ring_gather(piece, Z_HIGH, Y_UP, Y_DOWN)
    mine_x = jnp.concatenate([s[3] for s in sims], axis=0)
    other_x = send(mine_x, CORE)
    mine_p = jnp.concatenate([s[3] for s in pieces], axis=0)
    other_p = send(mine_p, CORE)

    offsets = lambda got: [(a, b, c, d.shape[0]) for a, b, c, d in got]
    of, op, ox = offsets(blocks), offsets(pieces), offsets(sims)
    n_f = len(blocks)
    anywhere = pl.BlockSpec(memory_space=pl.ANY)
    smem = pl.BlockSpec(memory_space=pltpu.SMEM)
    vmem = pl.BlockSpec(memory_space=pltpu.VMEM)
    f32 = jnp.float32
    cores, weights = pl.pallas_call(
        small_products(of, op, ox, n_f),
        out_shape=(jax.ShapeDtypeStruct((PANELS, WIN, WIN), f32), jax.ShapeDtypeStruct((J, SIMS_LOCAL), f32)),
        in_specs=[smem, smem, smem] + [anywhere] * (4 + n_f),
        out_specs=(vmem, vmem),
        scratch_shapes=[
            pltpu.VMEM((B, J), f32), pltpu.VMEM((B, J), f32), pltpu.VMEM((PANELS * B, SIMS_LOCAL), f32),
            pltpu.SemaphoreType.DMA((n_f + 2 * len(op) + 2 * len(ox),)),
        ],
        name="small_products",
    )(pos, keep_c, keep_r, mine_p, other_p, mine_x, other_x, *[b[3] for b in blocks])

    steps = 6
    tall = B // steps
    wide = lambda shape: pl.BlockSpec(shape, lambda i: (i, 0))
    whole = lambda shape: pl.BlockSpec(shape, lambda i: (0,) * len(shape))
    updated, conditioned = pl.pallas_call(
        large_products(of, op, n_f, steps),
        grid=(steps,),
        out_shape=(jax.ShapeDtypeStruct((B, B), f32), jax.ShapeDtypeStruct((B, SIMS_LOCAL), f32)),
        in_specs=[smem, wide((tall, B)), wide((tall, SIMS_LOCAL)), whole((PANELS, WIN, WIN)), whole((J, SIMS_LOCAL))]
        + [anywhere] * (2 + n_f),
        out_specs=(wide((tall, B)), wide((tall, SIMS_LOCAL))),
        scratch_shapes=[
            pltpu.VMEM((B, J), f32), pltpu.VMEM((B, J), f32),
            pltpu.VMEM((B, J), jnp.bfloat16), pltpu.VMEM((B, J), jnp.bfloat16),
            pltpu.SemaphoreType.DMA((n_f + 2 * len(op),)),
        ],
        name="large_products",
    )(pos, trailing, trailing_sims, cores, weights, mine_p, other_p, *[b[3] for b in blocks])
    return updated, conditioned


def solution(mesh):
    return jax.shard_map(
        on_device,
        mesh=mesh,
        in_specs=(P("row", "col"), P("col", "row", None), P("col", "row", None), P(), P("col", "row"), P("col", "row")),
        out_specs=(P("row", "col"), P("col", "row")),
        check_vma=False,
    )
```
